256 devices in a mesh: section: 8 (over x, core), fsdp: 16 (over y_hi, z), dp: 2 (over y_lo).
Axes of the slice: x: 4, y: 4 (y_hi: 2, y_lo: 2; y = y_hi * 2 + y_lo), z: 8, core: 2. Of those that a mesh axis runs over, the one named last changes fastest.
Arguments:
- section_inputs: bfloat16 [8, 2, 2048, 4096], P('section', 'dp', 'fsdp'), may hold values from -6 to 6
- queries: bfloat16 [8, 2, 2048, 4096], P('section', 'dp', 'fsdp'), may hold values from -110 to 110
- keys: bfloat16 [8, 2, 2048, 1024], P('section', 'dp', 'fsdp'), may hold values from -4.5 to 4.5
- w_value: bfloat16 [8, 4096, 1024], P('section', 'fsdp'), may hold values from -0.09375 to 0.09375
- gain: bfloat16 [8, 4096], P('section', 'fsdp'), may hold values from 0.5 to 1.5
- section_grads_in: bfloat16 [8, 2, 2048, 4096], P('section', 'dp', 'fsdp'), may hold values from -6 to 6
Outputs:
- passed_grads: bfloat16 [8, 2, 2048, 4096], P('section', 'dp', 'fsdp')
- w_value_grad: bfloat16 [8, 4096, 1024], P('section', ('fsdp', 'dp'))
- gain_grad: float32 [8, 4096], P('section', ('fsdp', 'dp'))
The draws below stay inside these ranges and needn't reach their ends.
All inputs are finite; a program needn't handle non-finite values.
Results may differ from the reference program's by a relative error of at most 0.029.
Values may be sent and summed in bfloat16 or wider, within the bound.
A program may use at most 64 MiB of HBM per device.

```python
import jax
import jax.numpy as jnp
from jax import lax

D = 4096
QH = 32
KVH = 8
DH = 128
MEM = 128
TOK_DEV = 128
GROUP = 4
KV = 1024
TOKENS = 2048
SECTIONS = 8
DOCS = 2
N_FSDP = 16


def paired_draw(key):
    base = jax.random.fold_in(key, 101)
    key_draw = jax.random.fold_in(base, 1)
    query_draw = jax.random.fold_in(base, 2)
    key_rows = jnp.clip(jax.random.normal(key_draw, (SECTIONS, DOCS, TOKENS, KVH * DH), jnp.float32), -4.0, 4.0)
    query_rows = jnp.clip(jax.random.normal(query_draw, (SECTIONS, DOCS, TOKENS, QH * DH), jnp.float32), -4.0, 4.0)
    return (key_rows, query_rows)


def draw_queries(key, part):
    return paired_draw(key)[1].astype(jnp.bfloat16)


def draw_keys(key, part):
    return paired_draw(key)[0].astype(jnp.bfloat16)


def strengthened(drawn, stream_key, source, target, shards_of, factor):
    def block_of(axis_at):
        return (jnp.arange(drawn.shape[axis_at]) // (drawn.shape[axis_at] // shards_of)).reshape((-1,) + (1,) * (drawn.ndim - 1 - axis_at))

    near = jax.random.permutation(stream_key, shards_of)[block_of(target)]
    other_side = (block_of(target) + shards_of // 2) % shards_of
    return jnp.where((block_of(source) == near) | (block_of(source) == other_side), factor * drawn, drawn)


def block_scale(key, shape, shards, smallest, high):
    def one(position, shards_of):
        heights = jax.random.uniform(jax.random.fold_in(jax.random.fold_in(key, 6), position), (shards_of,), jnp.float32, smallest / len(shards), high / len(shards))
        return jnp.repeat(jnp.exp(heights), shape[position] // shards_of).reshape((-1,) + (1,) * (len(shape) - position - 1))

    factor_of = one(*shards[0])
    for cut in shards[1:]:
        factor_of = factor_of * one(*cut)
    return factor_of


def gaussian(key, dims, scale, reach, pieces=(), kind=jnp.bfloat16):
    values = jax.random.normal(key, dims, jnp.float32) * scale
    if len(pieces) > 0:
        values = block_scale(key, dims, pieces, -0.22, 0.18) * values
    return jnp.clip(values, min=-reach, max=reach).astype(kind)


def noise_with(rng, dims, deviation, reach, pieces, heavy, kind=jnp.bfloat16):
    values = deviation * jax.random.normal(rng, dims, jnp.float32)
    if pieces:
        values = values * block_scale(rng, dims, pieces, -0.22, 0.18)
    return jnp.clip(strengthened(values, jax.random.fold_in(rng, 3), *heavy), -reach, reach).astype(kind)


def setup_inputs(seed: int = 0) -> dict:
    key_list = jax.random.split(jax.random.key(seed), 7)
    section_inputs = noise_with(key_list[0], (SECTIONS, DOCS, TOKENS, D), 1.0, 6.0, ((0, 8), (1, 2), (2, 16)), (2, 3, 16, 2.0))
    queries = draw_queries(jax.random.fold_in(key_list[6], 71), 0)
    keys = draw_keys(jax.random.fold_in(key_list[6], 71), 0)
    w_value = gaussian(key_list[3], (SECTIONS, D, KV), D ** -0.5, 0.09375, ((0, 8), (1, 16)))
    gain = jnp.clip(1.0 + 0.1 * jax.random.normal(key_list[4], (SECTIONS, D), jnp.float32), 0.5, 1.5).astype(jnp.bfloat16)
    section_grads_in = gaussian(key_list[5], (SECTIONS, DOCS, TOKENS, D), 1.0, 6.0, ((0, 8), (1, 2), (2, 16)))
    return dict(section_inputs=section_inputs, queries=queries, keys=keys, w_value=w_value, gain=gain, section_grads_in=section_grads_in)


NEG_FILL = -1e+30
EPSILON = 1e-05

def section_backward(inputs, queries, keys, weight, gain, cotangent):
    wide = inputs.astype(jnp.float32)
    inv_rms = lax.rsqrt(lax.optimization_barrier(jnp.mean(wide * wide, axis=1, keepdims=True)) + EPSILON)
    normed = wide * inv_rms
    gain_float = gain.astype(jnp.float32)
    normed_b = (normed * gain_float).astype(jnp.bfloat16)
    positions = jnp.arange(TOKENS, dtype=jnp.int32)
    visible = (positions[None, :] <= positions[:, None]) | (positions[None, :] < MEM)
    query_groups = queries.reshape(TOKENS, KVH, GROUP, DH).transpose(1, 2, 0, 3)
    key_groups = keys.reshape(TOKENS, KVH, DH).transpose(1, 0, 2)
    grad_groups = cotangent.reshape(N_FSDP, TOK_DEV, KVH, GROUP, DH).transpose(2, 0, 1, 3, 4)

    def group_values(operands):
        query_group, key_group, grad_group = operands
        scores = jnp.einsum('htd,kd->htk', query_group.astype(jnp.float32), key_group.astype(jnp.float32)) * DH ** (-0.5)
        scores = jnp.where(visible[None], scores, NEG_FILL)
        rounded_probs = lax.optimization_barrier(jax.nn.softmax(scores, axis=2).astype(jnp.bfloat16))
        blocks = rounded_probs.astype(jnp.float32).reshape(GROUP, N_FSDP, TOK_DEV, TOKENS)
        partial_value = jnp.einsum('hftk,fthd->fkd', blocks, grad_group.astype(jnp.float32))
        rounded = lax.optimization_barrier(partial_value.astype(jnp.bfloat16))
        return lax.optimization_barrier(jnp.sum(rounded.astype(jnp.float32), axis=0))
    value_grad = lax.map(group_values, (query_groups, key_groups, grad_groups))
    value_grad = value_grad.transpose(1, 0, 2).reshape(TOKENS, KVH * DH).astype(jnp.bfloat16)
    normed_grad = jnp.dot(value_grad, weight.T, preferred_element_type=jnp.float32)
    scaled = normed_grad * gain_float
    inner_mean = lax.optimization_barrier(jnp.mean(scaled * normed, axis=1, keepdims=True))
    input_grad = (cotangent.astype(jnp.float32) + inv_rms * (scaled - normed * inner_mean)).astype(jnp.bfloat16)
    gain_terms = lax.optimization_barrier(jnp.sum((normed_grad * normed).reshape(N_FSDP, TOK_DEV, D), axis=1))
    gain_terms = lax.optimization_barrier(gain_terms.astype(jnp.bfloat16)).astype(jnp.float32)
    weight_terms = jnp.einsum('ftd,ftk->fdk', normed_b.reshape(N_FSDP, TOK_DEV, D).astype(jnp.float32), value_grad.reshape(N_FSDP, TOK_DEV, KVH * DH).astype(jnp.float32))
    weight_terms = lax.optimization_barrier(weight_terms.astype(jnp.bfloat16)).astype(jnp.float32)
    return (input_grad, lax.optimization_barrier(jnp.sum(weight_terms, axis=0)), lax.optimization_barrier(jnp.sum(gain_terms, axis=0)))

def reference(section_inputs, queries, keys, w_value, gain, section_grads_in):
    input_list = []
    weight_list = []
    gain_list = []
    for section_index in range(SECTIONS):
        weight_sum = jnp.zeros((D, KVH * DH), jnp.float32)
        gain_sum = jnp.zeros((D,), jnp.float32)
        produced = []
        for doc_index in range(DOCS):
            input_grad, weight_terms, gain_terms = section_backward(section_inputs[section_index, doc_index], queries[section_index, doc_index], keys[section_index, doc_index], w_value[section_index], gain[section_index], section_grads_in[section_index, doc_index])
            produced.append(input_grad)
            weight_sum = weight_sum + weight_terms
            gain_sum = gain_sum + gain_terms
        input_list.append(jnp.stack(produced))
        weight_list.append(weight_sum.astype(jnp.bfloat16))
        gain_list.append(gain_sum)
    input_stack = jnp.stack(input_list)
    passed = jnp.concatenate([input_stack[1:], input_stack[:1]], axis=0)
    return (passed, jnp.stack(weight_list), jnp.stack(gain_list))
```

```python
import functools
import math

import jax
import jax.numpy as jnp
from jax import lax
from jax.experimental import pallas as pl
from jax.experimental.pallas import tpu as pltpu
from jax.sharding import PartitionSpec as P

MESH = pl.DeviceIdType.MESH
BF16, F32 = jnp.bfloat16, jnp.float32

NY = 4
NZ = 8
TOK = 128
D = 4096
KV = 1024
DH = 128
GROUP = 4
QC = D // NY
KC = KV // NY
GL = KC // DH
WID = GROUP * TOK
CHUNKS = 4
ROWS = TOK // CHUNKS

NEG_FILL = -1e30
EPSILON = 1e-05
EXP_SCALE = DH ** (-0.5) * math.log2(math.e)

NT = (((1,), (1,)), ((), ()))


def kernel(
    x_hbm, q_hbm, k_hbm, w_hbm, gain_ref, dy_hbm,
    passed_hbm, wout_ref, gout_ref,
    xfull, dyfull, qb, dyb, xb, kall, wall,
    irms, gtile, gall, mref, lref, term,
    vsend, vrecv, vgs, vgall,
    normt, wsend, wrecv, usend, urecv, outb, gsend, grecv, gpart,
    loc, ys, yr, kxs, kxr, wxs, wxr, vs, vr, ws, wr, us, ur, ps, pr, gs, gr, hs, hr,
):
    sec = lax.axis_index("section")
    fsdp = lax.axis_index("fsdp")
    dp = lax.axis_index("dp")
    n_sec = lax.axis_size("section")
    row = fsdp // NZ
    z = lax.rem(fsdp, NZ)
    c = row * 2 + dp

    def at(cy, cz):
        return (sec, (cy // 2) * NZ + cz, lax.rem(cy, 2))

    def ypeer(o):
        return lax.rem(c + o, NY)

    def zoff(o):
        return lax.rem(z + (o + NZ), NZ)

    def lanes(start, size):
        return pl.ds(pl.multiple_of(start, 128), size)

    below = (lax.rem(sec + (n_sec - 1), n_sec), fsdp, dp)
    above = (lax.rem(sec + 1, n_sec), fsdp, dp)

    barrier = pltpu.get_barrier_semaphore()
    for o in range(1, NY):
        pl.semaphore_signal(barrier, inc=1, device_id=at(ypeer(o), z), device_id_type=MESH)
    for o in range(1, NZ):
        pl.semaphore_signal(barrier, inc=1, device_id=at(c, zoff(o)), device_id_type=MESH)
    pl.semaphore_signal(barrier, inc=1, device_id=below, device_id_type=MESH)
    pl.semaphore_signal(barrier, inc=1, device_id=above, device_id_type=MESH)

    sent = []

    def remote(src, dst, ssem, rsem, device):
        return pltpu.make_async_remote_copy(
            src_ref=src, dst_ref=dst, send_sem=ssem, recv_sem=rsem,
            device_id=device, device_id_type=MESH,
        )

    def send(*args):
        copy = remote(*args)
        copy.start()
        sent.append(copy)
        return copy

    def feature(part, piece):
        return lanes((part // 2) * (D // 2) + piece * 256 + lax.rem(part, 2) * 128, 128)

    x_local = pltpu.make_async_copy(x_hbm, xfull, loc.at[0])
    k_local = pltpu.make_async_copy(k_hbm.at[:, lanes(c * KC, KC)], kall.at[z, c], loc.at[1])
    q_local = pltpu.make_async_copy(q_hbm.at[:, lanes(c * QC, QC)], qb.at[c], loc.at[2])
    dyc_local = pltpu.make_async_copy(dy_hbm.at[:, lanes(c * QC, QC)], dyb.at[c], loc.at[3])
    w_local = pltpu.make_async_copy(w_hbm.at[lanes(dp * 128, 128), :], wall.at[z], loc.at[4])
    dy_local = pltpu.make_async_copy(dy_hbm, dyfull, loc.at[5])
    for copy in (k_local, w_local, x_local, q_local, dyc_local, dy_local):
        copy.start()

    half = jnp.where(dp == 0, gain_ref[:, 0:128].astype(F32), gain_ref[:, 128:256].astype(F32))
    gtile[...] = jnp.broadcast_to(half, (8, 128))

    pl.semaphore_wait(barrier, (NY - 1) + (NZ - 1) + 2)

    def k_send(o):
        pc = ypeer(o)
        return (k_hbm.at[:, lanes(pc * KC, KC)], kall.at[z, c], ys.at[0, o - 1], yr.at[0, o - 1], at(pc, z))

    def q_send(o):
        pc = ypeer(o)
        return (q_hbm.at[:, lanes(pc * QC, QC)], qb.at[c], ys.at[1, o - 1], yr.at[1, o - 1], at(pc, z))

    def dy_send(o):
        pc = ypeer(o)
        return (dy_hbm.at[:, lanes(pc * QC, QC)], dyb.at[c], ys.at[2, o - 1], yr.at[2, o - 1], at(pc, z))

    order = (2, 1, 3)
    k_recv = {o: send(*k_send(o)) for o in order}
    def ring_send(buf, step, way, halves, size, ssem, rsem):
        block = zoff(-step) if way == 0 else zoff(step)
        target = at(c, zoff(1) if way == 0 else zoff(-1))
        out = []
        for h in halves:
            ref = buf.at[block, pl.ds(h * size, size)]
            out.append(send(ref, ref, ssem.at[way, step, h], rsem.at[way, step, h], target))
        return out

    def ring_wait(buf, step, way, halves, size, ssem, rsem):
        block = zoff(-1 - step) if way == 0 else zoff(1 + step)
        for h in halves:
            ref = buf.at[block, pl.ds(h * size, size)]
            remote(ref, ref, ssem.at[way, step, h], rsem.at[way, step, h], at(c, zoff(1))).wait_recv()

    def halves_of(step, way):
        if step < 3:
            return (0, 1)
        return (0,) if way == 0 else (1,)

    def ag_send(which, step):
        buf, size, ssem, rsem = which
        for way in (0, 1):
            ring_send(buf, step, way, halves_of(step, way), size, ssem, rsem)

    def ag_wait(which, step):
        buf, size, ssem, rsem = which
        for way in (0, 1):
            ring_wait(buf, step, way, halves_of(step, way), size, ssem, rsem)

    kring = (kall, 2, kxs, kxr)
    wring = (wall, 64, wxs, wxr)

    w_local.wait()
    ag_send(wring, 0)
    q_recv = {o: send(*q_send(o)) for o in order}
    dy_recv = {o: send(*dy_send(o)) for o in order}
    for o in range(1, NZ):
        send(gtile, gall.at[z], gs.at[o - 1], gr.at[o - 1], at(c, zoff(o)))
    gall[z] = gtile[...]

    for o in order:
        k_recv[o].wait_recv()
    k_local.wait()
    ag_send(kring, 0)

    x_whole = {}
    for o in order:
        pc = ypeer(o)
        for piece in range(NZ):
            remote(
                x_hbm.at[:, feature(pc, piece)], xb.at[c, :, pl.ds(piece * 128, 128)],
                ys.at[3, o - 1], yr.at[3, o - 1], at(pc, z),
            ).start()
        x_whole[o] = remote(xb.at[c], xb.at[c], ys.at[3, o - 1], yr.at[3, o - 1], at(pc, z))
    x_local.wait()
    for piece in range(NZ):
        xb[c, :, piece * 128:(piece + 1) * 128] = xfull[:, feature(c, piece)]
    squares = jnp.zeros((TOK, 128), F32)
    for col in range(D // 128):
        v = xfull[:, col * 128:(col + 1) * 128].astype(F32)
        squares = squares + v * v
    rms = lax.rsqrt(jnp.sum(squares, axis=1, keepdims=True) * (1.0 / D) + EPSILON)
    irms[c] = jnp.broadcast_to(rms, (TOK, 128))
    r_recv = {
        o: send(irms.at[c], irms.at[c], ys.at[4, o - 1], yr.at[4, o - 1], at(ypeer(o), z)) for o in order
    }

    mref[...] = jnp.full_like(mref, NEG_FILL)
    lref[...] = jnp.zeros_like(lref)

    def stack(buf, src, g):
        return jnp.concatenate(
            [buf[src, :, lanes(g * WID + h * DH, DH)] for h in range(GROUP)], axis=0
        )

    def scores(src, block, ksrc, g):
        k = kall[block, ksrc, :, lanes(g * DH, DH)]
        return lax.dot_general(k, stack(qb, src, g), NT, preferred_element_type=F32)

    def diagonal(s, open_all):
        key = lax.broadcasted_iota(jnp.int32, (TOK, WID), 0)
        tok = lax.rem(lax.broadcasted_iota(jnp.int32, (TOK, WID), 1), TOK)
        seen = key <= tok
        if open_all is not None:
            seen = seen | open_all
        return jnp.where(seen, s, NEG_FILL)

    def update(idx, s):
        s = s.reshape(TOK // 8, 8, WID)
        old = mref[idx]
        new = jnp.maximum(old, jnp.max(s, axis=0))
        p = jnp.exp2((s - new[None]) * EXP_SCALE)
        lref[idx] = lref[idx] * jnp.exp2((old - new) * EXP_SCALE) + jnp.sum(p, axis=0)
        mref[idx] = new

    def pass_one(block, own):
        def body(j, carry):
            d, g = j // GL, lax.rem(j, GL)
            update(4 + j, scores(2 + d, block, d, g))

            def lower():
                a = scores(2 + d, block, 2 + d, g)
                b = scores(d, block, d, g)
                if own:
                    a = diagonal(a, None)
                    b = diagonal(b, z == 0)
                update(4 + j, a)
                update(j, b)

            if own:
                lower()
            else:
                pl.when(block <= z)(lower)
            return carry

        lax.fori_loop(0, 2 * GL, body, 0)

    def finish_stats():
        for idx in range(8):
            m8 = mref[idx]
            m = jnp.max(m8, axis=0, keepdims=True)
            total = jnp.sum(lref[idx] * jnp.exp2((m8 - m) * EXP_SCALE), axis=0, keepdims=True)
            mref[idx] = jnp.broadcast_to(m * EXP_SCALE + jnp.log(total) * math.log2(math.e), (8, WID))

    def weights(idx, s):
        p = jnp.exp2(s.reshape(TOK // 8, 8, WID) * EXP_SCALE - mref[idx][None])
        return p.reshape(TOK, WID).astype(BF16)

    def pass_two(slot, block, own):
        def body(j, carry):
            d, g = j // GL, lax.rem(j, GL)
            dy1 = stack(dyb, 2 + d, g)
            p = weights(4 + j, scores(2 + d, block, d, g))
            upper = jnp.dot(p, dy1, preferred_element_type=F32)

            def lower():
                a = scores(2 + d, block, 2 + d, g)
                b = scores(d, block, d, g)
                if own:
                    a = diagonal(a, None)
                    b = diagonal(b, z == 0)
                pa = weights(4 + j, a)
                pb = weights(j, b)
                term[slot, 2 + d, :, lanes(g * DH, DH)] = jnp.dot(pa, dy1, preferred_element_type=F32)
                term[slot, d, :, lanes(g * DH, DH)] = upper + jnp.dot(
                    pb, stack(dyb, d, g), preferred_element_type=F32
                )

            def upper_only():
                term[slot, 2 + d, :, lanes(g * DH, DH)] = jnp.zeros((TOK, DH), F32)
                term[slot, d, :, lanes(g * DH, DH)] = upper

            if own:
                lower()
            else:
                pl.when(block <= z)(lower)
                pl.when(block > z)(upper_only)
            return carry

        lax.fori_loop(0, 2 * GL, body, 0)

    ag_wait(kring, 0)
    ag_send(kring, 1)
    ag_wait(kring, 1)
    ag_send(kring, 2)
    for o in order:
        q_recv[o].wait_recv()
    q_local.wait()
    pass_one(z, True)
    pass_one(zoff(-1), False)
    pass_one(zoff(1), False)
    ag_wait(kring, 2)
    ag_send(kring, 3)
    ag_wait(wring, 0)
    ag_send(wring, 1)
    pass_one(zoff(-2), False)
    pass_one(zoff(2), False)
    pass_one(zoff(-3), False)
    pass_one(zoff(3), False)
    ag_wait(kring, 3)
    pass_one(zoff(4), False)
    finish_stats()

    for o in order:
        dy_recv[o].wait_recv()
    dyc_local.wait()

    def rs_args(sbuf, rbuf, ssem, rsem, step, way, h, size):
        return (
            sbuf.at[way, step, pl.ds(h * size, size)], rbuf.at[way, step, pl.ds(h * size, size)],
            ssem.at[way, step, h], rsem.at[way, step, h], at(c, zoff(1) if way == 0 else zoff(-1)),
        )

    def started(step, way, h):
        return step > 0 or h == way

    def rs_step(own_of, sbuf, rbuf, ssem, rsem, step, size):
        for way in (0, 1):
            for h in (0, 1):
                if not started(step, way, h):
                    continue
                part = pl.ds(h * size, size)
                value = own_of(way, part)
                if step > 0 and started(step - 1, way, h):
                    remote(*rs_args(sbuf, rbuf, ssem, rsem, step - 1, way, h, size)).wait_recv()
                    value = value + rbuf[way, step - 1, part].astype(F32)
                sbuf[way, step, part] = value.astype(BF16)
                send(*rs_args(sbuf, rbuf, ssem, rsem, step, way, h, size))

    def rs_last(own_of, sbuf, rbuf, ssem, rsem, h, size):
        part = pl.ds(h * size, size)
        value = own_of(0, part)
        for way in (0, 1):
            remote(*rs_args(sbuf, rbuf, ssem, rsem, 3, way, h, size)).wait_recv()
            value = value + rbuf[way, 3, part].astype(F32)
        return value

    def term_of(way, part):
        return term[way, part]

    pass_two(0, zoff(4), False)
    rs_step(lambda way, part: term[0, part], vsend, vrecv, vs, vr, 0, 2)
    for step in (1, 2, 3):
        pass_two(0, zoff(4 - step), False)
        pass_two(1, zoff(step - 4), False)
        rs_step(term_of, vsend, vrecv, vs, vr, step, 2)
        if step == 2:
            for o in order:
                x_whole[o].wait_recv()
                r_recv[o].wait_recv()
            for o in range(1, NZ):
                src = zoff(-o)
                remote(gtile, gall.at[src], gs.at[o - 1], gr.at[o - 1], at(c, src)).wait_recv()

            def norm_body(piece, carry):
                gain_row = gall[piece, 0:1, :]
                for src in range(NY):
                    xhat = xb[src, :, lanes(piece * 128, 128)].astype(F32) * irms[src]
                    normed = (xhat * gain_row).astype(BF16)
                    normt[piece, :, src * TOK:(src + 1) * TOK] = normed.T
                return carry

            lax.fori_loop(0, NZ, norm_body, 0)
    pass_two(0, z, True)
    for h in (0, 1):
        vgs[h * 2:h * 2 + 2] = rs_last(term_of, vsend, vrecv, vs, vr, h, 2).astype(BF16)
    v_recv = {
        o: send(vgs, vgall.at[:, :, lanes(c * KC, KC)], ys.at[5, o - 1], yr.at[5, o - 1], at(ypeer(o), z))
        for o in order
    }
    vgall[:, :, lanes(c * KC, KC)] = vgs[...]
    ag_wait(wring, 1)
    ag_send(wring, 2)
    ag_wait(wring, 2)
    ag_send(wring, 3)
    for o in order:
        src = ypeer(NY - o)
        remote(vgs, vgall.at[:, :, lanes(src * KC, KC)], ys.at[5, o - 1], yr.at[5, o - 1], at(src, z)).wait_recv()

    def weight_part(slot, piece):
        vg = vgall[...].reshape(NY * TOK, KV)
        term2 = jnp.dot(normt[piece], vg, preferred_element_type=F32)
        return term2

    def wpiece(step):
        low = weight_part(0, zoff(4 - step))
        high = low if step == 0 else weight_part(1, zoff(step - 4))
        return lambda way, part: (low, high)[way][part.start:part.start + part.size]

    rs_step(wpiece(0), wsend, wrecv, ws, wr, 0, 64)

    ag_wait(wring, 3)
    gain_wide = jnp.concatenate([gall[i, 0:1, :] for i in range(NZ)], axis=1)
    gpart[...] = jnp.zeros_like(gpart)
    weight_all = wall[...].reshape(NZ * 128, KV)

    for o in (2, 1, 3, 0):
        src = ypeer(o)
        ng = lax.dot_general(vgall[src], weight_all, NT, preferred_element_type=F32)
        usend[src] = (ng * gain_wide).astype(BF16)
        rr = irms[src]
        for piece in range(NZ):
            cols = slice(piece * 128, (piece + 1) * 128)
            prod = ng[:, cols] * (xb[src, :, cols].astype(F32) * rr)
            gpart[:, cols] += jnp.sum(prod.reshape(TOK // 8, 8, 128), axis=0)
    for t in range(CHUNKS):
        part = pl.ds(t * ROWS, ROWS)
        for o in order:
            src = ypeer(o)
            send(usend.at[src, part], urecv.at[c, part], us.at[o - 1, t], ur.at[o - 1, t], at(src, z))
    for piece in range(NZ):
        total = jnp.sum(gpart[:, piece * 128:(piece + 1) * 128], axis=0, keepdims=True)
        gsend[piece] = jnp.broadcast_to(total, (8, 128))
    for o in range(1, NZ):
        send(gsend.at[zoff(o)], grecv.at[o], hs.at[o - 1], hr.at[o - 1], at(c, zoff(o)))
    dy_local.wait()

    def finalize(t):
        part = pl.ds(t * ROWS, ROWS)
        for o in order:
            src = ypeer(NY - o)
            remote(
                usend.at[src, part], urecv.at[src, part], us.at[o - 1, t], ur.at[o - 1, t], at(src, z)
            ).wait_recv()
        urecv[c, part] = usend[c, part]
        rr = irms[c, part]
        acc = jnp.zeros((ROWS, 128), F32)
        for src in range(NY):
            for piece in range(NZ):
                base = (src // 2) * (D // 2) + piece * 256 + (src % 2) * 128
                xhat = xfull[part, base:base + 128].astype(F32) * rr
                acc = acc + urecv[src, part, piece * 128:(piece + 1) * 128].astype(F32) * xhat
        m = jnp.sum(acc, axis=1, keepdims=True) * (1.0 / D)
        for src in range(NY):
            for piece in range(NZ):
                base = (src // 2) * (D // 2) + piece * 256 + (src % 2) * 128
                xhat = xfull[part, base:base + 128].astype(F32) * rr
                u = urecv[src, part, piece * 128:(piece + 1) * 128].astype(F32)
                grad = dyfull[part, base:base + 128].astype(F32) + rr * (u - xhat * m)
                outb[part, base:base + 128] = grad.astype(BF16)
        send(outb.at[part], passed_hbm.at[part], ps.at[t], pr.at[t], below)

    rs_step(wpiece(1), wsend, wrecv, ws, wr, 1, 64)
    finalize(0)
    finalize(1)
    rs_step(wpiece(2), wsend, wrecv, ws, wr, 2, 64)
    finalize(2)
    finalize(3)
    rs_step(wpiece(3), wsend, wrecv, ws, wr, 3, 64)
    gtotal = gsend[z]
    for o in range(1, NZ):
        remote(gsend.at[z], grecv.at[o], hs.at[o - 1], hr.at[o - 1], at(c, zoff(o))).wait_recv()
        gtotal = gtotal + grecv[o]
    gout_ref[...] = gtotal[0:1]
    last = weight_part(0, z)
    for h in (0, 1):
        value = rs_last(lambda way, part: last[part.start:part.start + part.size], wsend, wrecv, ws, wr, h, 64)
        wout_ref[h * 64:(h + 1) * 64] = value.astype(BF16)
    for t in range(CHUNKS):
        part = pl.ds(t * ROWS, ROWS)
        remote(outb.at[part], passed_hbm.at[part], ps.at[t], pr.at[t], below).wait_recv()
    for o in order:
        x_whole[o].wait_send()
    for copy in sent:
        copy.wait_send()


def per_device(section_inputs, queries, keys, w_value, gain, section_grads_in):
    dma = pltpu.SemaphoreType.DMA
    vmem = pltpu.VMEM
    any_space = pl.BlockSpec(memory_space=pl.ANY)
    in_vmem = pl.BlockSpec(memory_space=pltpu.VMEM)
    passed, weight, gains = pl.pallas_call(
        kernel,
        out_shape=(
            jax.ShapeDtypeStruct((TOK, D), BF16),
            jax.ShapeDtypeStruct((TOK, KV), BF16),
            jax.ShapeDtypeStruct((1, 128), F32),
        ),
        in_specs=[any_space, any_space, any_space, any_space, in_vmem, any_space],
        out_specs=(any_space, in_vmem, in_vmem),
        scratch_shapes=[
            vmem((TOK, D), BF16),
            vmem((TOK, D), BF16),
            vmem((NY, TOK, QC), BF16),
            vmem((NY, TOK, QC), BF16),
            vmem((NY, TOK, QC), BF16),
            vmem((NZ, NY, TOK, KC), BF16),
            vmem((NZ, 128, KV), BF16),
            vmem((NY, TOK, 128), F32),
            vmem((8, 128), F32),
            vmem((NZ, 8, 128), F32),
            vmem((8, 8, WID), F32),
            vmem((8, 8, WID), F32),
            vmem((2, NY, TOK, KC), F32),
            vmem((2, 4, NY, TOK, KC), BF16),
            vmem((2, 4, NY, TOK, KC), BF16),
            vmem((NY, TOK, KC), BF16),
            vmem((NY, TOK, KV), BF16),
            vmem((NZ, 128, NY * TOK), BF16),
            vmem((2, 4, 128, KV), BF16),
            vmem((2, 4, 128, KV), BF16),
            vmem((NY, TOK, QC), BF16),
            vmem((NY, TOK, QC), BF16),
            vmem((TOK, D), BF16),
            vmem((NZ, 8, 128), F32),
            vmem((NZ, 8, 128), F32),
            vmem((8, QC), F32),
            dma((6,)),
            dma((6, 3)), dma((6, 3)),
            dma((2, 4, 2)), dma((2, 4, 2)),
            dma((2, 4, 2)), dma((2, 4, 2)),
            dma((2, 4, 2)), dma((2, 4, 2)),
            dma((2, 4, 2)), dma((2, 4, 2)),
            dma((3, CHUNKS)), dma((3, CHUNKS)),
            dma((CHUNKS,)), dma((CHUNKS,)),
            dma((NZ - 1,)), dma((NZ - 1,)),
            dma((NZ - 1,)), dma((NZ - 1,)),
        ],
        compiler_params=pltpu.CompilerParams(
            collective_id=0, has_side_effects=True, vmem_limit_bytes=60 * 1024 * 1024
        ),
        name="tick",
    )(section_inputs[0, 0], queries[0, 0], keys[0, 0], w_value[0], gain, section_grads_in[0, 0])
    return passed[None, None], weight[None], gains


def solution(mesh):
    return jax.shard_map(
        per_device,
        mesh=mesh,
        in_specs=(
            P("section", "dp", "fsdp", None),
            P("section", "dp", "fsdp", None),
            P("section", "dp", "fsdp", None),
            P("section", "fsdp", None),
            P("section", "fsdp"),
            P("section", "dp", "fsdp", None),
        ),
        out_specs=(
            P("section", "dp", "fsdp", None),
            P("section", ("fsdp", "dp"), None),
            P("section", ("fsdp", "dp")),
        ),
        check_vma=False,
    )
```

```python
import functools
import math

import jax
import jax.numpy as jnp
from jax import lax
from jax.experimental import pallas as pl
from jax.experimental.pallas import tpu as pltpu
from jax.sharding import PartitionSpec as P

MESH = pl.DeviceIdType.MESH
BF16, F32 = jnp.bfloat16, jnp.float32

NY = 4
NZ = 8
TOK = 128
D = 4096
KV = 1024
DH = 128
GROUP = 4
QC = D // NY
KC = KV // NY
GL = KC // DH
WID = GROUP * TOK
CHUNKS = 4
ROWS = TOK // CHUNKS

NEG_FILL = -1e30
EPSILON = 1e-05
EXP_SCALE = DH ** (-0.5) * math.log2(math.e)

NT = (((1,), (1,)), ((), ()))


def kernel(
    x_hbm, q_hbm, k_hbm, w_hbm, gain_ref, dy_hbm,
    passed_hbm, wout_ref, gout_ref,
    xfull, dyfull, qb, dyb, xb, kall, wall,
    irms, gtile, gall, mref, lref, term,
    vsend, vrecv, vgs, vgall,
    normt, wsend, wrecv, usend, urecv, outb, gsend, grecv, gpart,
    loc, ys, yr, kxs, kxr, wxs, wxr, vs, vr, ws, wr, us, ur, ps, pr, gs, gr, hs, hr,
):
    sec = lax.axis_index("section")
    fsdp = lax.axis_index("fsdp")
    dp = lax.axis_index("dp")
    n_sec = lax.axis_size("section")
    row = fsdp // NZ
    z = lax.rem(fsdp, NZ)
    c = row * 2 + dp

    def at(cy, cz):
        return (sec, (cy // 2) * NZ + cz, lax.rem(cy, 2))

    def ypeer(o):
        return lax.rem(c + o, NY)

    def zoff(o):
        return lax.rem(z + (o + NZ), NZ)

    def lanes(start, size):
        return pl.ds(pl.multiple_of(start, 128), size)

    below = (lax.rem(sec + (n_sec - 1), n_sec), fsdp, dp)
    above = (lax.rem(sec + 1, n_sec), fsdp, dp)

    barrier = pltpu.get_barrier_semaphore()
    for o in range(1, NY):
        pl.semaphore_signal(barrier, inc=1, device_id=at(ypeer(o), z), device_id_type=MESH)
    for o in (1, -1):
        pl.semaphore_signal(barrier, inc=1, device_id=at(c, zoff(o)), device_id_type=MESH)
    pl.semaphore_signal(barrier, inc=1, device_id=below, device_id_type=MESH)
    pl.semaphore_signal(barrier, inc=1, device_id=above, device_id_type=MESH)

    sent = []

    def remote(src, dst, ssem, rsem, device):
        return pltpu.make_async_remote_copy(
            src_ref=src, dst_ref=dst, send_sem=ssem, recv_sem=rsem,
            device_id=device, device_id_type=MESH,
        )

    def send(*args):
        copy = remote(*args)
        copy.start()
        sent.append(copy)
        return copy

    def feature(part, piece):
        return lanes((part // 2) * (D // 2) + piece * 256 + lax.rem(part, 2) * 128, 128)

    x_local = pltpu.make_async_copy(x_hbm, xfull, loc.at[0])
    k_local = pltpu.make_async_copy(k_hbm.at[:, lanes(c * KC, KC)], kall.at[z, c], loc.at[1])
    q_local = pltpu.make_async_copy(q_hbm.at[:, lanes(c * QC, QC)], qb.at[c], loc.at[2])
    dyc_local = pltpu.make_async_copy(dy_hbm.at[:, lanes(c * QC, QC)], dyb.at[c], loc.at[3])
    w_local = pltpu.make_async_copy(w_hbm.at[lanes(dp * 128, 128), :], wall.at[z], loc.at[4])
    dy_local = pltpu.make_async_copy(dy_hbm, dyfull, loc.at[5])
    for copy in (k_local, w_local, x_local, q_local, dyc_local, dy_local):
        copy.start()

    half = jnp.where(dp == 0, gain_ref[:, 0:128].astype(F32), gain_ref[:, 128:256].astype(F32))
    gtile[...] = jnp.broadcast_to(half, (8, 128))

    pl.semaphore_wait(barrier, (NY - 1) + 2 + 2)

    def k_send(o):
        pc = ypeer(o)
        return (k_hbm.at[:, lanes(pc * KC, KC)], kall.at[z, c], ys.at[0, o - 1], yr.at[0, o - 1], at(pc, z))

    def q_send(o):
        pc = ypeer(o)
        return (q_hbm.at[:, lanes(pc * QC, QC)], qb.at[c], ys.at[1, o - 1], yr.at[1, o - 1], at(pc, z))

    def dy_send(o):
        pc = ypeer(o)
        return (dy_hbm.at[:, lanes(pc * QC, QC)], dyb.at[c], ys.at[2, o - 1], yr.at[2, o - 1], at(pc, z))

    order = (2, 1, 3)
    k_recv = {o: send(*k_send(o)) for o in order}
    def ring_args(ring, step, way, part, block):
        ref_of, _, ssem, rsem = ring
        ref = ref_of(block, part)
        target = at(c, zoff(1) if way == 0 else zoff(-1))
        return (ref, ref, ssem.at[way, step, part], rsem.at[way, step, part], target)

    def steps_of(way, part):
        return 4 if way == part % 2 else 3

    def ring_open(ring, part):
        for way in (0, 1):
            send(*ring_args(ring, 0, way, part, z))

    def ring_pass(ring, step):
        for part in range(ring[1]):
            for way in (0, 1):
                if step < steps_of(way, part):
                    block = zoff(-1 - step) if way == 0 else zoff(1 + step)
                    remote(*ring_args(ring, step, way, part, block)).wait_recv()
                    if step + 1 < steps_of(way, part):
                        send(*ring_args(ring, step + 1, way, part, block))

    around = (0, 1, 3, 2)

    def k_part(block, part):
        return kall.at[block, ypeer(NY - around[part])]

    def w_part(block, part):
        return wall.at[block, pl.ds(part * 64, 64)]

    def g_part(block, part):
        return gall.at[block]

    kring = (k_part, 4, kxs, kxr)
    wring = (w_part, 2, wxs, wxr)
    gring = (g_part, 1, gs, gr)

    k_local.wait()
    ring_open(kring, 0)
    w_local.wait()
    ring_open(wring, 0)
    q_recv = {o: send(*q_send(o)) for o in order}
    dy_recv = {o: send(*dy_send(o)) for o in order}
    gall[z] = gtile[...]
    for part in (1, 2, 3):
        k_recv[around[part]].wait_recv()
        ring_open(kring, part)
    for way in (0, 1):
        target = at(c, zoff(1) if way == 0 else zoff(-1))
        send(gtile, gall.at[z], gs.at[way, 0, 0], gr.at[way, 0, 0], target)

    x_whole = {}
    for o in order:
        pc = ypeer(o)
        for piece in range(NZ):
            remote(
                x_hbm.at[:, feature(pc, piece)], xb.at[c, :, pl.ds(piece * 128, 128)],
                ys.at[3, o - 1], yr.at[3, o - 1], at(pc, z),
            ).start()
        x_whole[o] = remote(xb.at[c], xb.at[c], ys.at[3, o - 1], yr.at[3, o - 1], at(pc, z))
    x_local.wait()
    for piece in range(NZ):
        xb[c, :, piece * 128:(piece + 1) * 128] = xfull[:, feature(c, piece)]
    squares = jnp.zeros((TOK, 128), F32)
    for col in range(D // 128):
        v = xfull[:, col * 128:(col + 1) * 128].astype(F32)
        squares = squares + v * v
    rms = lax.rsqrt(jnp.sum(squares, axis=1, keepdims=True) * (1.0 / D) + EPSILON)
    irms[c] = jnp.broadcast_to(rms, (TOK, 128))
    r_recv = {
        o: send(irms.at[c], irms.at[c], ys.at[4, o - 1], yr.at[4, o - 1], at(ypeer(o), z)) for o in order
    }

    mref[...] = jnp.full_like(mref, NEG_FILL)
    lref[...] = jnp.zeros_like(lref)

    def head(buf, src, g, h):
        return buf[src, :, lanes(g * WID + h * DH, DH)]

    def key_rows(block, ksrc, g):
        return kall[block, ksrc, :, lanes(g * DH, DH)]

    def scores(k, src, g, h):
        return lax.dot_general(k, head(qb, src, g, h), NT, preferred_element_type=F32)

    def seen_of(open_all):
        key = lax.broadcasted_iota(jnp.int32, (TOK, TOK), 0)
        seen = key <= lax.broadcasted_iota(jnp.int32, (TOK, TOK), 1)
        return seen if open_all is None else seen | open_all

    def update(idx, h, s):
        cols = slice(h * TOK, (h + 1) * TOK)
        s = s.reshape(s.shape[0] // 8, 8, TOK)
        old = mref[idx, :, cols]
        new = jnp.maximum(old, jnp.max(s, axis=0))
        p = jnp.exp2((s - new[None]) * EXP_SCALE)
        lref[idx, :, cols] = lref[idx, :, cols] * jnp.exp2((old - new) * EXP_SCALE) + jnp.sum(p, axis=0)
        mref[idx, :, cols] = new

    def repeat(body):
        lax.fori_loop(0, 2 * GL, body, 0, unroll=2)

    def pass_one(block, own):
        def full(j, carry):
            d, g = j // GL, lax.rem(j, GL)
            k0, k1 = key_rows(block, d, g), key_rows(block, 2 + d, g)
            both = jnp.concatenate([k0, k1], axis=0)
            for h in range(GROUP):
                a = scores(both, 2 + d, g, h)
                b = scores(k0, d, g, h)
                if own:
                    low = jnp.where(seen_of(None), a[TOK:], NEG_FILL)
                    a = jnp.concatenate([a[:TOK], low], axis=0)
                    b = jnp.where(seen_of(z == 0), b, NEG_FILL)
                update(4 + j, h, a)
                update(j, h, b)
            return carry

        def light(j, carry):
            d, g = j // GL, lax.rem(j, GL)
            k0 = key_rows(block, d, g)
            for h in range(GROUP):
                update(4 + j, h, scores(k0, 2 + d, g, h))
            return carry

        if own:
            repeat(full)
        else:
            pl.when(block <= z)(lambda: repeat(full))
            pl.when(block > z)(lambda: repeat(light))

    def finish_stats():
        for idx in range(8):
            m8 = mref[idx]
            m = jnp.max(m8, axis=0, keepdims=True)
            total = jnp.sum(lref[idx] * jnp.exp2((m8 - m) * EXP_SCALE), axis=0, keepdims=True)
            mref[idx] = jnp.broadcast_to(m * EXP_SCALE + jnp.log(total) * math.log2(math.e), (8, WID))

    def weights(idx, h, s):
        cols = slice(h * TOK, (h + 1) * TOK)
        p = jnp.exp2(s.reshape(s.shape[0] // 8, 8, TOK) * EXP_SCALE - mref[idx, :, cols][None])
        return p.reshape(s.shape).astype(BF16)

    def cotangents(src, g):
        return jnp.concatenate([head(dyb, src, g, h) for h in range(GROUP)], axis=0)

    def pass_two(slot, block, own):
        def full(j, carry):
            d, g = j // GL, lax.rem(j, GL)
            k0, k1 = key_rows(block, d, g), key_rows(block, 2 + d, g)
            both = jnp.concatenate([k0, k1], axis=0)
            pa, pb = [], []
            for h in range(GROUP):
                a = scores(both, 2 + d, g, h)
                b = scores(k0, d, g, h)
                if own:
                    low = jnp.where(seen_of(None), a[TOK:], NEG_FILL)
                    a = jnp.concatenate([a[:TOK], low], axis=0)
                    b = jnp.where(seen_of(z == 0), b, NEG_FILL)
                pa.append(weights(4 + j, h, a))
                pb.append(weights(j, h, b))
            upper = jnp.dot(jnp.concatenate(pa, axis=1), cotangents(2 + d, g), preferred_element_type=F32)
            lower = jnp.dot(jnp.concatenate(pb, axis=1), cotangents(d, g), preferred_element_type=F32)
            term[slot, d, :, lanes(g * DH, DH)] = upper[:TOK] + lower
            term[slot, 2 + d, :, lanes(g * DH, DH)] = upper[TOK:]
            return carry

        def light(j, carry):
            d, g = j // GL, lax.rem(j, GL)
            k0 = key_rows(block, d, g)
            pa = [weights(4 + j, h, scores(k0, 2 + d, g, h)) for h in range(GROUP)]
            term[slot, d, :, lanes(g * DH, DH)] = jnp.dot(
                jnp.concatenate(pa, axis=1), cotangents(2 + d, g), preferred_element_type=F32
            )
            term[slot, 2 + d, :, lanes(g * DH, DH)] = jnp.zeros((TOK, DH), F32)
            return carry

        if own:
            repeat(full)
        else:
            pl.when(block <= z)(lambda: repeat(full))
            pl.when(block > z)(lambda: repeat(light))

    ring_pass(kring, 0)
    ring_pass(gring, 0)
    ring_pass(kring, 1)
    for o in order:
        q_recv[o].wait_recv()
    q_local.wait()
    pass_one(z, True)
    pass_one(zoff(-1), False)
    ring_pass(kring, 2)
    ring_pass(gring, 1)
    ring_open(wring, 1)
    pass_one(zoff(1), False)
    pass_one(zoff(-2), False)
    ring_pass(kring, 3)
    ring_pass(wring, 0)
    pass_one(zoff(2), False)
    pass_one(zoff(-3), False)
    pass_one(zoff(3), False)
    pass_one(zoff(4), False)
    finish_stats()

    for o in order:
        dy_recv[o].wait_recv()
    dyc_local.wait()

    def rs_args(sbuf, rbuf, ssem, rsem, step, way, h, size):
        return (
            sbuf.at[way, step, pl.ds(h * size, size)], rbuf.at[way, step, pl.ds(h * size, size)],
            ssem.at[way, step, h], rsem.at[way, step, h], at(c, zoff(1) if way == 0 else zoff(-1)),
        )

    def started(step, way, h):
        return step > 0 or h == way

    def rs_step(own_of, sbuf, rbuf, ssem, rsem, step, size):
        for way, h in ((0, 1), (1, 0), (0, 0), (1, 1)):
            if not started(step, way, h):
                continue
            part = pl.ds(h * size, size)
            value = own_of(way, part)
            if step > 0 and started(step - 1, way, h):
                remote(*rs_args(sbuf, rbuf, ssem, rsem, step - 1, way, h, size)).wait_recv()
                value = value + rbuf[way, step - 1, part].astype(F32)
            sbuf[way, step, part] = value.astype(BF16)
            send(*rs_args(sbuf, rbuf, ssem, rsem, step, way, h, size))

    def rs_last(own_of, sbuf, rbuf, ssem, rsem, h, size):
        part = pl.ds(h * size, size)
        value = own_of(0, part)
        for way in (0, 1):
            remote(*rs_args(sbuf, rbuf, ssem, rsem, 3, way, h, size)).wait_recv()
            value = value + rbuf[way, 3, part].astype(F32)
        return value

    def term_of(way, part):
        return term[way, part]

    pass_two(0, zoff(4), False)
    rs_step(lambda way, part: term[0, part], vsend, vrecv, vs, vr, 0, 2)
    for step in (1, 2, 3):
        pass_two(0, zoff(4 - step), False)
        pass_two(1, zoff(step - 4), False)
        rs_step(term_of, vsend, vrecv, vs, vr, step, 2)
        if step < 3:
            ring_pass(wring, step)
        if step == 2:
            for o in order:
                x_whole[o].wait_recv()
                r_recv[o].wait_recv()
            ring_pass(gring, 2)
            ring_pass(gring, 3)

            def norm_body(piece, carry):
                gain_row = gall[piece, 0:1, :]
                for src in range(NY):
                    xhat = xb[src, :, lanes(piece * 128, 128)].astype(F32) * irms[src]
                    normed = (xhat * gain_row).astype(BF16)
                    normt[piece, :, src * TOK:(src + 1) * TOK] = normed.T
                return carry

            lax.fori_loop(0, NZ, norm_body, 0)
    pass_two(0, z, True)
    def v_args(h, o, src):
        rows = pl.ds(2 * h, 2)
        return (
            vgs.at[rows], vgall.at[rows, :, lanes(src * KC, KC)],
            ys.at[5 + h, o - 1], yr.at[5 + h, o - 1], at(ypeer(o), z),
        )

    def v_wait(h, o):
        remote(*v_args(h, o, ypeer(NY - o))).wait_recv()

    for h in (0, 1):
        half = rs_last(term_of, vsend, vrecv, vs, vr, h, 2).astype(BF16)
        vgs[2 * h:2 * h + 2] = half
        for o in order:
            send(*v_args(h, o, c))
        vgall[2 * h:2 * h + 2, :, lanes(c * KC, KC)] = half

    def weight_part(piece, q):
        cols = lanes(ypeer(NY - around[q]) * KC, KC)
        return jnp.dot(normt[piece], vgall[:, :, cols].reshape(NY * TOK, KC), preferred_element_type=F32)

    def w_args(step, way, q):
        return (
            wsend.at[way, step, q], wrecv.at[way, step, q], ws.at[way, step, q], wr.at[way, step, q],
            at(c, zoff(1) if way == 0 else zoff(-1)),
        )

    def w_step(q, step):
        for way in (1 - q % 2, q % 2):
            first = 0 if way == q % 2 else 1
            if step < first:
                continue
            value = weight_part(zoff(4 - step) if way == 0 else zoff(step - 4), q)
            if step > first:
                remote(*w_args(step - 1, way, q)).wait_recv()
                value = value + wrecv[way, step - 1, q].astype(F32)
            wsend[way, step, q] = value.astype(BF16)
            send(*w_args(step, way, q))

    def w_last(q):
        value = weight_part(z, q)
        for way in (0, 1):
            remote(*w_args(3, way, q)).wait_recv()
            value = value + wrecv[way, 3, q].astype(F32)
        wout_ref[:, lanes(ypeer(NY - around[q]) * KC, KC)] = value.astype(BF16)

    def g_args(step, way):
        return (
            gsend.at[way, step], grecv.at[way, step], hs.at[way, step], hr.at[way, step],
            at(c, zoff(1) if way == 0 else zoff(-1)),
        )

    def g_own(piece):
        return gpart[piece]

    def g_step(step):
        for way in (1, 0):
            if step < way:
                continue
            value = g_own(zoff(4 - step) if way == 0 else zoff(step - 4))
            if step > way:
                remote(*g_args(step - 1, way)).wait_recv()
                value = value + grecv[way, step - 1]
            gsend[way, step] = value
            send(*g_args(step, way))

    gain_wide = jnp.concatenate([gall[i, 0:1, :] for i in range(NZ)], axis=1)

    def u_args(src, t):
        part = pl.ds(t * ROWS, ROWS)
        o = lax.rem(src - c + NY, NY)
        return (usend.at[src, part], urecv.at[c, part], us.at[src, t], ur.at[o, t], at(src, z))

    def u_step(src):
        weight_all = wall[...].reshape(NZ * 128, KV)
        ng = lax.dot_general(vgall[src], weight_all, NT, preferred_element_type=F32)
        usend[src] = (ng * gain_wide).astype(BF16)

        @pl.when(c != src)
        def _():
            for t in range(CHUNKS):
                remote(*u_args(src, t)).start()

        rr = irms[src]
        for piece in range(NZ):
            cols = slice(piece * 128, (piece + 1) * 128)
            prod = ng[:, cols] * (xb[src, :, cols].astype(F32) * rr)
            total = jnp.sum(prod.reshape(TOK // 8, 8, 128), axis=0)
            gpart[piece] = total if src == 0 else gpart[piece] + total

    w_step(0, 0)
    ring_pass(wring, 3)
    w_step(0, 1)
    for o in order:
        v_wait(0, o)
    u_step(0)
    u_step(1)
    w_step(0, 2)
    for q in (1, 2, 3):
        v_wait(1, around[q])
        w_step(q, 0)
    u_step(2)
    u_step(3)
    g_step(0)
    dy_local.wait()

    def finalize(t):
        part = pl.ds(t * ROWS, ROWS)
        for o in order:
            src = ypeer(NY - o)
            remote(
                usend.at[src, part], urecv.at[src, part], us.at[src, t], ur.at[o, t], at(src, z)
            ).wait_recv()
        urecv[c, part] = usend[c, part]
        rr = irms[c, part]
        acc = jnp.zeros((ROWS, 128), F32)
        for src in range(NY):
            for piece in range(NZ):
                base = (src // 2) * (D // 2) + piece * 256 + (src % 2) * 128
                xhat = xfull[part, base:base + 128].astype(F32) * rr
                acc = acc + urecv[src, part, piece * 128:(piece + 1) * 128].astype(F32) * xhat
        m = jnp.sum(acc, axis=1, keepdims=True) * (1.0 / D)
        for src in range(NY):
            for piece in range(NZ):
                base = (src // 2) * (D // 2) + piece * 256 + (src % 2) * 128
                xhat = xfull[part, base:base + 128].astype(F32) * rr
                u = urecv[src, part, piece * 128:(piece + 1) * 128].astype(F32)
                grad = dyfull[part, base:base + 128].astype(F32) + rr * (u - xhat * m)
                outb[part, base:base + 128] = grad.astype(BF16)
        send(outb.at[part], passed_hbm.at[part], ps.at[t], pr.at[t], below)

    w_step(0, 3)
    for q in (1, 2, 3):
        w_step(q, 1)
    g_step(1)
    for q in (1, 2, 3):
        w_step(q, 2)
    g_step(2)
    finalize(0)
    for q in (1, 2, 3):
        w_step(q, 3)
    g_step(3)
    finalize(1)
    finalize(2)
    finalize(3)
    gtotal = g_own(z)
    for way in (0, 1):
        remote(*g_args(3, way)).wait_recv()
        gtotal = gtotal + grecv[way, 3]
    gout_ref[...] = jnp.sum(gtotal, axis=0, keepdims=True)
    for q in range(NY):
        w_last(q)
    for t in range(CHUNKS):
        part = pl.ds(t * ROWS, ROWS)
        remote(outb.at[part], passed_hbm.at[part], ps.at[t], pr.at[t], below).wait_recv()
    for o in order:
        x_whole[o].wait_send()
    for copy in sent:
        copy.wait_send()
    for src in range(NY):
        @pl.when(c != src)
        def _():
            for t in range(CHUNKS):
                remote(*u_args(src, t)).wait_send()


def per_device(section_inputs, queries, keys, w_value, gain, section_grads_in):
    dma = pltpu.SemaphoreType.DMA
    vmem = pltpu.VMEM
    any_space = pl.BlockSpec(memory_space=pl.ANY)
    in_vmem = pl.BlockSpec(memory_space=pltpu.VMEM)
    passed, weight, gains = pl.pallas_call(
        kernel,
        out_shape=(
            pltpu.VMEM((TOK, D), BF16),
            pltpu.VMEM((TOK, KV), BF16),
            pltpu.VMEM((1, 128), F32),
        ),
        in_specs=[any_space, any_space, any_space, any_space, in_vmem, any_space],
        out_specs=(in_vmem, in_vmem, in_vmem),
        scratch_shapes=[
            vmem((TOK, D), BF16),
            vmem((TOK, D), BF16),
            vmem((NY, TOK, QC), BF16),
            vmem((NY, TOK, QC), BF16),
            vmem((NY, TOK, QC), BF16),
            vmem((NZ, NY, TOK, KC), BF16),
            vmem((NZ, 128, KV), BF16),
            vmem((NY, TOK, 128), F32),
            vmem((8, 128), F32),
            vmem((NZ, 8, 128), F32),
            vmem((8, 8, WID), F32),
            vmem((8, 8, WID), F32),
            vmem((2, NY, TOK, KC), F32),
            vmem((2, 4, NY, TOK, KC), BF16),
            vmem((2, 4, NY, TOK, KC), BF16),
            vmem((NY, TOK, KC), BF16),
            vmem((NY, TOK, KV), BF16),
            vmem((NZ, 128, NY * TOK), BF16),
            vmem((2, 4, NY, 128, KC), BF16),
            vmem((2, 4, NY, 128, KC), BF16),
            vmem((NY, TOK, QC), BF16),
            vmem((NY, TOK, QC), BF16),
            vmem((TOK, D), BF16),
            vmem((2, 4, 8, 128), F32),
            vmem((2, 4, 8, 128), F32),
            vmem((NZ, 8, 128), F32),
            dma((6,)),
            dma((7, 3)), dma((7, 3)),
            dma((2, 4, 4)), dma((2, 4, 4)),
            dma((2, 4, 2)), dma((2, 4, 2)),
            dma((2, 4, 2)), dma((2, 4, 2)),
            dma((2, 4, 4)), dma((2, 4, 4)),
            dma((NY, CHUNKS)), dma((NY, CHUNKS)),
            dma((CHUNKS,)), dma((CHUNKS,)),
            dma((2, 4, 1)), dma((2, 4, 1)),
            dma((2, 4)), dma((2, 4)),
        ],
        compiler_params=pltpu.CompilerParams(
            collective_id=0, has_side_effects=True, vmem_limit_bytes=60 * 1024 * 1024
        ),
        name="tick",
    )(section_inputs[0, 0], queries[0, 0], keys[0, 0], w_value[0], gain, section_grads_in[0, 0])
    return passed[None, None], weight[None], gains


def solution(mesh):
    return jax.shard_map(
        per_device,
        mesh=mesh,
        in_specs=(
            P("section", "dp", "fsdp", None),
            P("section", "dp", "fsdp", None),
            P("section", "dp", "fsdp", None),
            P("section", "fsdp", None),
            P("section", "fsdp"),
            P("section", "dp", "fsdp", None),
        ),
        out_specs=(
            P("section", "dp", "fsdp", None),
            P("section", ("fsdp", "dp"), None),
            P("section", ("fsdp", "dp")),
        ),
        check_vma=False,
    )
```
